512 devices in a mesh: row: 8 (over x, y_lo), col: 4 (over y_hi, core), seq: 16 (over z).
Axes of the slice: x: 4, y: 4 (y_hi: 2, y_lo: 2; y = y_hi * 2 + y_lo), z: 16, core: 2. Of those that a mesh axis runs over, the one named last changes fastest.
Arguments:
- hidden_in: bfloat16 [8, 3072, 6144], P('row', 'seq', 'col'), may hold values from -6 to 6
- projection: bfloat16 [6144, 9216], P(('col', 'seq'), 'row'), may hold values from -0.078125 to 0.078125
Outputs:
- attention: bfloat16 [8, 3072, 3072], P('col', 'seq', 'row')
The draws below stay inside these ranges and needn't reach their ends.
All inputs are finite; a program needn't handle non-finite values.
Results may differ from the reference program's by a relative error of at most 0.012.
Values may be sent and summed in bfloat16 or wider, within the bound.
A program may use at most 64 MiB of HBM per device.

```python
import math
import jax
import jax.numpy as jnp
from jax import lax

D = 6144
HEADS = 24
HD = 128
BATCH = 8
LS = 192
LEN = 3072
N_COL = 4
N_SEQ = 16


def draw_hidden_in(key, part):
    noise_key = jax.random.fold_in(key, 11)
    sign_key = jax.random.fold_in(key, 12)
    noise = jax.random.normal(noise_key, (BATCH, LEN, D), jnp.float32)
    signs = (2 * jax.random.randint(sign_key, (D,), 0, 2) - 1).astype(jnp.float32)
    places = jnp.arange(LEN, dtype=jnp.int32)
    offset = (places % LS).astype(jnp.float32)
    slope = (2.0 * offset + 1.0 - LS) * (4.0 / LS)
    slope = jnp.where(places >= LS, slope, 0.0)
    values = noise + slope[None, :, None] * signs[None, None, :]
    return jnp.clip(values, -6.0, 6.0).astype(jnp.bfloat16)


def level_of(stream_key, extent, cuts, smallest, top_value):
    factor_of = 1.0
    for dim, shards_of in cuts:
        draws = jax.random.uniform(jax.random.fold_in(jax.random.fold_in(stream_key, 6), dim), (shards_of,), jnp.float32, smallest / len(cuts), top_value / len(cuts))
        factor_of = factor_of * jnp.repeat(jnp.exp(draws), extent[dim] // shards_of).reshape((-1,) + (1,) * (len(extent) - 1 - dim))
    return factor_of


def normal_values(key, dims, scale, most, cuts=(), kind=jnp.bfloat16):
    values = jax.random.normal(key, dims, jnp.float32) * scale
    if len(cuts) > 0:
        values = level_of(key, dims, cuts, -0.22, 0.18) * values
    return jnp.clip(values, min=-most, max=most).astype(kind)


def setup_inputs(seed: int = 0) -> dict:
    arg_keys = jax.random.split(jax.random.key(seed), 3)
    hidden_in = draw_hidden_in(jax.random.fold_in(arg_keys[2], 71), 0)
    projection = normal_values(arg_keys[1], (D, 3 * HEADS * HD), D ** -0.5, 0.078125, ((0, 64), (1, 8)))
    return {"hidden_in": hidden_in, "projection": projection}


def feature_map(rows, angle, factor):
    active = jnp.maximum(rows.astype(jnp.float32), 0.0)
    cosine = jnp.cos(angle)[None, :, None, None]
    sine = jnp.sin(angle)[None, :, None, None]
    joined = jnp.concatenate([active * cosine, active * sine], axis=-1) * factor
    return lax.optimization_barrier(joined.astype(jnp.bfloat16))


def reference(hidden_in, projection):
    panel_rows = D // N_COL

    def project_one(sequence):
        totals = jnp.zeros((LEN, 3 * HEADS * HD), jnp.float32)
        for column in range(N_COL):
            part = jnp.dot(sequence[:, column * panel_rows:(column + 1) * panel_rows],
                           projection[column * panel_rows:(column + 1) * panel_rows],
                           preferred_element_type=jnp.float32)
            rounded = lax.optimization_barrier(part.astype(jnp.bfloat16))
            totals = totals + rounded.astype(jnp.float32)
        return lax.optimization_barrier(totals.astype(jnp.bfloat16))

    projected = lax.map(project_one, hidden_in).reshape(BATCH, LEN, HEADS, 3, HD)
    positions = jnp.arange(LEN, dtype=jnp.int32).astype(jnp.float32)
    angle = positions * (0.5 * math.pi / LEN)
    query_feat = feature_map(projected[:, :, :, 0], angle, HD ** -0.5)
    key_feat = feature_map(projected[:, :, :, 1], angle, 1.0)
    values = projected[:, :, :, 2]

    def blocks(array):
        return jnp.moveaxis(array.reshape((BATCH, N_SEQ, LS) + array.shape[2:]), 1, 0)

    causal = jnp.tril(jnp.ones((LS, LS), jnp.bool_))

    def step(carry, block):
        state, norm = carry
        query_blk, key_blk, value_blk = block
        query_wide = query_blk.astype(jnp.float32)
        key_wide = key_blk.astype(jnp.float32)
        value_wide = value_blk.astype(jnp.float32)
        scores = jnp.einsum('bihf,bjhf->bhij', query_wide, key_wide)
        masked = jnp.where(causal, scores, 0.0)
        weights = lax.optimization_barrier(masked.astype(jnp.bfloat16))
        numerator = jnp.einsum('bhij,bjhd->bihd', weights.astype(jnp.float32), value_wide)
        numerator = numerator + jnp.einsum('bihf,bhfd->bihd', query_wide, state, precision=lax.Precision.HIGHEST)
        denominator = jnp.sum(masked, axis=-1) + jnp.einsum('bihf,bhf->bhi', query_wide, norm, precision=lax.Precision.HIGHEST)
        denominator = jnp.maximum(denominator, 1.0)
        output = (numerator / jnp.transpose(denominator, (0, 2, 1))[..., None]).astype(jnp.bfloat16)
        state = state + jnp.einsum('bjhf,bjhd->bhfd', key_wide, value_wide)
        norm = norm + jnp.sum(key_wide, axis=1)
        return (state, norm), output

    start = (jnp.zeros((BATCH, HEADS, 2 * HD, HD), jnp.float32), jnp.zeros((BATCH, HEADS, 2 * HD), jnp.float32))
    final, outputs = lax.scan(step, start, (blocks(query_feat), blocks(key_feat), blocks(values)))
    return jnp.moveaxis(outputs, 0, 1).reshape(BATCH, LEN, HEADS * HD)
```

```python
import functools
import math

import jax
import jax.numpy as jnp
from jax import lax
from jax.experimental import pallas as pl
from jax.experimental.pallas import tpu as pltpu
from jax.sharding import PartitionSpec as P

HD = 128
NX = 4
CHUNK = 96
QSTART = 4
MESH = pl.DeviceIdType.MESH
BF = jnp.bfloat16
F32 = jnp.float32


def dot(a, b, dims=((1,), (0,))):
    return lax.dot_general(a, b, (dims, ((), ())), preferred_element_type=F32)


def kernel(
    nseq, hid, proj, cos_ref, sin_ref, out,
    a_buf, wkv, wq, acc_f, acc_h, cs_kv, cs_q, cr_kv, cr_q, ys_kv, ys_q, yr_kv, yr_q,
    pkv, kf_buf, vx_buf, qf_buf, nd_buf, own, rb, ob,
    loc, y_s, y_r, x_s, x_r, z_s, z_r, c_s, c_r, h_s, h_r, p_s, p_r,
):
    length = hid.shape[1]
    half = length // 2
    shard = proj.shape[0]
    zhalf = shard // 2
    heads = proj.shape[1] // (3 * HD)
    r = lax.axis_index("row")
    c = lax.axis_index("col")
    z = lax.axis_index("seq")
    x, yl = r // 2, r % 2
    yh, core = c // 2, c % 2
    right = lax.rem(x + 1, NX) * 2 + yl
    left = lax.rem(x + NX - 1, NX) * 2 + yl
    ypart = x * 2 + (1 - yl)
    up = lax.rem(z + 1, nseq)
    down = lax.rem(z + nseq - 1, nseq)
    c1 = 2 * yh + (1 - core)
    c2 = 2 * (1 - yh) + core
    c3 = 2 * (1 - yh) + (1 - core)

    loads = [pltpu.make_async_copy(hid.at[0], a_buf.at[0, yl], loc.at[0])]
    mine = pl.ds(pl.multiple_of(z * shard, shard), shard)
    for h in range(heads):
        loads.append(pltpu.make_async_copy(
            proj.at[:, (3 * h + 1) * HD:(3 * h + 3) * HD], wkv.at[mine, 2 * h * HD:2 * (h + 1) * HD], loc.at[1 + 2 * h]))
        loads.append(pltpu.make_async_copy(
            proj.at[:, 3 * h * HD:(3 * h + 1) * HD], wq.at[mine, h * HD:(h + 1) * HD], loc.at[2 + 2 * h]))
    for ld in loads:
        ld.start()

    barrier = pltpu.get_barrier_semaphore()
    peers = [{"row": right}, {"row": left}, {"row": ypart}, {"seq": up}, {"seq": down}, {"col": c1}, {"col": c2}]
    for peer in peers:
        pl.semaphore_signal(barrier, inc=1, device_id=peer, device_id_type=MESH)
    for ld in loads:
        ld.wait()
    pl.semaphore_wait(barrier, len(peers))

    sent = []

    def send(src, dst, s_sem, r_sem, peer):
        cp = pltpu.make_async_remote_copy(src_ref=src, dst_ref=dst, send_sem=s_sem, recv_sem=r_sem,
                                          device_id=peer, device_id_type=MESH)
        cp.start()
        sent.append(cp)
        return cp

    rows_a, rows_b = slice(0, half), slice(half, length)
    yp = {"row": ypart}
    rt = {"row": right}
    lf = {"row": left}

    def z_src(way, step):
        owner = lax.rem(z + nseq - (step - 1), nseq) if way == 0 else lax.rem(z + step - 1, nseq)
        return owner * shard

    def z_ref(buf, way, step, part):
        return buf.at[pl.ds(pl.multiple_of(z_src(way, step) + part * zhalf, zhalf), zhalf)]

    last = nseq // 2
    z_copies = {}

    def z_used(way, step, part):
        return step < last or part == way

    def z_send(kind, step):
        buf = (wkv, wq)[kind]
        for part in range(2):
            for way in range(2):
                if z_used(way, step, part):
                    ref = z_ref(buf, way, step, part)
                    k = (kind, step - 1, way, part)
                    z_copies[k] = send(ref, ref, z_s.at[k], z_r.at[k], {"seq": up if way == 0 else down})

    def z_step(kind, step):
        buf = (wkv, wq)[kind]
        for part in range(2):
            for way in range(2):
                if z_used(way, step, part):
                    z_copies[(kind, step - 1, way, part)].wait_recv()
                    if step < last and z_used(way, step + 1, part):
                        ref = z_ref(buf, way, step + 1, part)
                        k = (kind, step, way, part)
                        z_copies[k] = send(ref, ref, z_s.at[k], z_r.at[k], {"seq": up if way == 0 else down})

    yl1 = 1 - yl
    z_send(0, 1)
    y0 = send(a_buf.at[0, yl, rows_a], a_buf.at[0, yl, rows_a], y_s.at[0], y_r.at[0], yp)
    r0 = send(a_buf.at[0, yl, rows_a], a_buf.at[3, yl, rows_a], x_s.at[0], x_r.at[0], rt)
    l0 = send(a_buf.at[0, yl, rows_b], a_buf.at[1, yl, rows_b], x_s.at[1], x_r.at[1], lf)
    y1 = send(a_buf.at[0, yl, rows_b], a_buf.at[0, yl, rows_b], y_s.at[1], y_r.at[1], yp)
    r1 = send(a_buf.at[0, yl, rows_b], a_buf.at[3, yl, rows_b], x_s.at[2], x_r.at[2], rt)
    l1 = send(a_buf.at[0, yl, rows_a], a_buf.at[1, yl, rows_a], x_s.at[3], x_r.at[3], lf)
    late = [r1, l1]
    for step in range(1, last + 1):
        z_step(0, step)
        if step == QSTART:
            z_send(1, 1)
        if step > QSTART:
            z_step(1, step - QSTART)
        if step == 2:
            r0.wait_recv()
            rf = send(a_buf.at[3, yl, rows_a], a_buf.at[2, yl, rows_a], x_s.at[4], x_r.at[4], rt)
            l0.wait_recv()
            lfw = send(a_buf.at[1, yl, rows_b], a_buf.at[2, yl, rows_b], x_s.at[5], x_r.at[5], lf)
        if step == 4:
            y0.wait_recv()
            y1.wait_recv()
            late.append(send(a_buf.at[0, yl1], a_buf.at[3, yl1], x_s.at[6], x_r.at[6], rt))
            late.append(send(a_buf.at[0, yl1], a_buf.at[1, yl1], x_s.at[7], x_r.at[7], lf))
        if step == 6:
            rf.wait_recv()
            late.append(send(a_buf.at[2, yl, rows_a], a_buf.at[2, yl, rows_a], y_s.at[2], y_r.at[2], yp))
            lfw.wait_recv()
            late.append(send(a_buf.at[2, yl, rows_b], a_buf.at[2, yl, rows_b], y_s.at[3], y_r.at[3], yp))
    q_next = last - QSTART + 1

    z_step(1, q_next)
    for cp in late:
        cp.wait_recv()
    z_step(1, q_next + 1)

    depth = a_buf.shape[3]

    def part_of(owner, w):
        j = lax.rem(owner + NX - x, NX)
        return dot(a_buf[j].reshape(2 * length, depth), w[...])

    core_peer = {"col": c1}
    far_peer = {"col": c2}

    def reduce_start(w, cs, cr, ys, yr, af, ah, k, between):
        cs[0] = part_of(c3, w).astype(BF)
        g0 = send(cs.at[0], cr.at[0], c_s.at[k, 0], c_r.at[k, 0], core_peer)
        af[...] = part_of(c2, w)
        between()
        g0.wait_recv()
        ys[...] = (af[...] + cr[0].astype(F32)).astype(BF)
        far = send(ys, yr, h_s.at[k], h_r.at[k], far_peer)
        cs[1] = part_of(c1, w).astype(BF)
        g1 = send(cs.at[1], cr.at[1], c_s.at[k, 1], c_r.at[k, 1], core_peer)
        ah[...] = part_of(c, w)
        return g1, far

    nkv = 2 * heads * HD
    acc_fk, acc_hk = acc_f.at[:, :nkv], acc_h.at[:, :nkv]
    acc_fq, acc_hq = acc_f.at[:, nkv:], acc_h.at[:, nkv:]
    g1, far = reduce_start(wkv, cs_kv, cr_kv, ys_kv, yr_kv, acc_fk, acc_hk, 0, lambda: z_step(1, q_next + 2))
    z_step(1, q_next + 3)
    g1q, farq = reduce_start(wq, cs_q, cr_q, ys_q, yr_q, acc_fq, acc_hq, 1, lambda: None)
    g1.wait_recv()
    far.wait_recv()
    pkv[...] = (acc_hk[...] + cr_kv[1].astype(F32) + yr_kv[...].astype(F32)).astype(BF)

    cosine, sine = cos_ref[...], sin_ref[...]
    ones8 = jnp.ones((8, length), BF)
    pairs = [(b, h) for b in range(2) for h in range(heads)]
    norms = len(pairs) * 2 * HD
    for i, (b, h) in enumerate(pairs):
        rows = slice(b * length, (b + 1) * length)
        key = jnp.maximum(pkv[rows, 2 * h * HD:(2 * h + 1) * HD].astype(F32), 0.0)
        val = pkv[rows, (2 * h + 1) * HD:(2 * h + 2) * HD]
        kc, ks = (key * cosine).astype(BF), (key * sine).astype(BF)
        kf_buf[i, :, :HD] = kc
        kf_buf[i, :, HD:] = ks
        vx_buf[i, :, :HD] = val
        vx_buf[i, :, HD:] = jnp.ones((length, HD), BF)
        at = i * 2 * HD
        own[at:at + HD] = dot(kc, val, ((0,), (0,)))
        own[at + HD:at + 2 * HD] = dot(ks, val, ((0,), (0,)))
        own[norms + 16 * i:norms + 16 * i + 8] = dot(ones8, kc)
        own[norms + 16 * i + 8:norms + 16 * i + 16] = dot(ones8, ks)

    def pass_on(i):
        rows = pl.ds(pl.multiple_of(i * CHUNK, CHUNK), CHUNK)
        return rows, pltpu.make_async_remote_copy(
            src_ref=ob.at[rows], dst_ref=rb.at[rows], send_sem=p_s.at[i], recv_sem=p_r.at[i],
            device_id={"seq": up}, device_id_type=MESH)

    chunks = rb.shape[0] // CHUNK

    def chain():
        @pl.loop(0, chunks)
        def _(i):
            rows, cp = pass_on(i)

            @pl.when(z > 0)
            def _():
                cp.wait_recv()

            @pl.when(z == 0)
            def _():
                rb[rows] = jnp.zeros((CHUNK, HD), BF)

            @pl.when(z < nseq - 1)
            def _():
                ob[rows] = (rb[rows].astype(F32) + own[rows]).astype(BF)
                cp.start()

    early = 4

    @pl.when(z < early)
    def _():
        chain()

    g1q.wait_recv()
    farq.wait_recv()
    acc_hq[...] = acc_hq[...] + cr_q[1].astype(F32) + yr_q[...].astype(F32)
    ii = lax.broadcasted_iota(jnp.int32, (length, length), 0)
    jj = lax.broadcasted_iota(jnp.int32, (length, length), 1)
    causal = jj <= ii
    for i, (b, h) in enumerate(pairs):
        rows = slice(b * length, (b + 1) * length)
        q = acc_hq[rows, h * HD:(h + 1) * HD].astype(BF).astype(F32)
        q = jnp.maximum(q, 0.0)
        qf_buf[i, :, :HD] = (q * cosine * HD ** -0.5).astype(BF)
        qf_buf[i, :, HD:] = (q * sine * HD ** -0.5).astype(BF)
        s = dot(qf_buf[i], kf_buf[i], ((1,), (1,)))
        wts = jnp.where(causal, s, 0.0).astype(BF)
        nd_buf[i] = dot(wts, vx_buf[i])

    @pl.when(z >= early)
    def _():
        chain()

    for i, (b, h) in enumerate(pairs):
        at = i * 2 * HD
        qf = qf_buf[i]
        num = nd_buf[i, :, :HD] + dot(qf, rb[at:at + 2 * HD])
        nc = rb[norms + 16 * i:norms + 16 * i + 16].astype(F32)
        nrm = jnp.concatenate(
            [jnp.broadcast_to(nc[0:1], (HD, HD)), jnp.broadcast_to(nc[8:9], (HD, HD))], axis=1).astype(BF)
        den = nd_buf[i, :, HD:] + dot(qf, nrm, ((1,), (1,)))
        out[b, :, h * HD:(h + 1) * HD] = (num / jnp.maximum(den, 1.0)).astype(BF)

    for cp in sent:
        cp.wait_send()

    @pl.when(z < nseq - 1)
    def _():
        @pl.loop(0, chunks)
        def _(i):
            pass_on(i)[1].wait_send()


def body(nseq, hidden_in, projection):
    length, depth = hidden_in.shape[1:]
    shard, width = projection.shape
    heads = width // (3 * HD)
    positions = (lax.axis_index("seq") * length + jnp.arange(length, dtype=jnp.int32)).astype(F32)
    angle = positions * (0.5 * math.pi / (nseq * length))
    cosine = jnp.broadcast_to(jnp.cos(angle)[:, None], (length, HD))
    sine = jnp.broadcast_to(jnp.sin(angle)[:, None], (length, HD))
    nkv, nq = 2 * heads * HD, heads * HD
    rows = 2 * length
    pairs = 2 * heads
    st = pairs * (2 * HD + 16)
    vm, dma = pltpu.VMEM, pltpu.SemaphoreType.DMA
    anywhere = pl.BlockSpec(memory_space=pl.ANY)
    vmem = pl.BlockSpec(memory_space=pltpu.VMEM)
    zsem = (2, nseq // 2, 2, 2)
    return pl.pallas_call(
        functools.partial(kernel, nseq),
        out_shape=jax.ShapeDtypeStruct((2, length, nq), BF),
        in_specs=[anywhere, anywhere, vmem, vmem],
        out_specs=vmem,
        scratch_shapes=[
            vm((NX, 2, length, depth), BF), vm((nseq * shard, nkv), BF), vm((nseq * shard, nq), BF),
            vm((rows, width), F32), vm((rows, width), F32),
            vm((2, rows, nkv), BF), vm((2, rows, nq), BF), vm((2, rows, nkv), BF), vm((2, rows, nq), BF),
            vm((rows, nkv), BF), vm((rows, nq), BF), vm((rows, nkv), BF), vm((rows, nq), BF),
            vm((rows, nkv), BF),
            vm((pairs, length, 2 * HD), BF), vm((pairs, length, 2 * HD), BF), vm((pairs, length, 2 * HD), BF),
            vm((pairs, length, 2 * HD), F32),
            vm((st, HD), F32), vm((st, HD), BF), vm((st, HD), BF),
            dma((1 + 2 * heads,)), dma((4,)), dma((4,)), dma((8,)), dma((8,)),
            dma(zsem), dma(zsem), dma((2, 2)), dma((2, 2)), dma((2,)), dma((2,)),
            dma((st // CHUNK,)), dma((st // CHUNK,)),
        ],
        compiler_params=pltpu.CompilerParams(
            collective_id=0, has_side_effects=True, vmem_limit_bytes=56 * 1024 * 1024),
    )(hidden_in, projection, cosine, sine)


def solution(mesh):
    placed = (P("row", "seq", "col"), P(("col", "seq"), "row"))
    return jax.shard_map(
        functools.partial(body, mesh.shape["seq"]), mesh=mesh, in_specs=placed,
        out_specs=P("col", "seq", "row"), check_vma=False)
```

```python
import functools
import math

import jax
import jax.numpy as jnp
from jax import lax
from jax.experimental import pallas as pl
from jax.experimental.pallas import tpu as pltpu
from jax.sharding import PartitionSpec as P

HD = 128
NX = 4
CHUNK = 96
NORM = 16
QSTART = 5
EARLY = 8
PIECES = (6, 6)
MESH = pl.DeviceIdType.MESH
BF = jnp.bfloat16
F32 = jnp.float32


def dot(a, b, dims=((1,), (0,))):
    return lax.dot_general(a, b, (dims, ((), ())), preferred_element_type=F32)


def kernel(
    nseq, hid, proj, out,
    a_buf, wkv, wq, acc_k, acc_q, cs_kv, cs_q, cr_kv, cr_q, ys_kv, ys_q, yr_kv, yr_q,
    trig, pkv, kf_buf, vx_buf, qf_buf, nd_buf, own, own0, rb, rb0, ob,
    loc, y_s, y_r, x_s, x_r, k_s, k_r, q_s, q_r, c_s, c_r, h_s, h_r, p_s, p_r, o_s, o_r, f_s, f_r,
):
    length = hid.shape[1]
    half = length // 2
    shard = proj.shape[0]
    heads = proj.shape[1] // (3 * HD)
    pairs = 2 * heads
    r = lax.axis_index("row")
    c = lax.axis_index("col")
    z = lax.axis_index("seq")
    x, yl = r // 2, r % 2
    yh, core = c // 2, c % 2
    right = lax.rem(x + 1, NX) * 2 + yl
    left = lax.rem(x + NX - 1, NX) * 2 + yl
    ypart = x * 2 + (1 - yl)
    up = lax.rem(z + 1, nseq)
    down = lax.rem(z + nseq - 1, nseq)
    c1 = 2 * yh + (1 - core)
    c2 = 2 * (1 - yh) + core
    c3 = 2 * (1 - yh) + (1 - core)

    loads = [pltpu.make_async_copy(hid.at[0], a_buf.at[0, yl], loc.at[0])]
    mine = pl.ds(pl.multiple_of(z * shard, shard), shard)
    for h in range(heads):
        loads.append(pltpu.make_async_copy(
            proj.at[:, (3 * h + 1) * HD:(3 * h + 3) * HD], wkv.at[mine, 2 * h * HD:2 * (h + 1) * HD], loc.at[1 + 2 * h]))
        loads.append(pltpu.make_async_copy(
            proj.at[:, 3 * h * HD:(3 * h + 1) * HD], wq.at[mine, h * HD:(h + 1) * HD], loc.at[2 + 2 * h]))
    for ld in loads:
        ld.start()

    barrier = pltpu.get_barrier_semaphore()
    peers = [{"row": right}, {"row": left}, {"row": ypart}, {"seq": up}, {"seq": down}, {"col": c1}, {"col": c2}]
    for peer in peers:
        pl.semaphore_signal(barrier, inc=1, device_id=peer, device_id_type=MESH)
    for ld in loads:
        ld.wait()
    pl.semaphore_wait(barrier, len(peers))

    sent = []

    def remote(src, dst, s_sem, r_sem, peer):
        return pltpu.make_async_remote_copy(src_ref=src, dst_ref=dst, send_sem=s_sem, recv_sem=r_sem,
                                            device_id=peer, device_id_type=MESH)

    def send(*what):
        cp = remote(*what)
        cp.start()
        sent.append(cp)
        return cp

    rows_a, rows_b = slice(0, half), slice(half, length)
    yp = {"row": ypart}
    rt = {"row": right}
    lf = {"row": left}

    last = nseq // 2
    z_copies = {}

    def z_used(kind, way, step, part):
        return step < last or (part < PIECES[kind] // 2) == (way == 0)

    def z_one(kind, way, step, part):
        size = shard // PIECES[kind]
        owner = lax.rem(z + nseq - (step - 1), nseq) if way == 0 else lax.rem(z + step - 1, nseq)
        ref = (wkv, wq)[kind].at[pl.ds(pl.multiple_of(owner * shard + part * size, size), size)]
        k = (step - 1, way, part)
        z_copies[(kind,) + k] = send(
            ref, ref, (k_s, q_s)[kind].at[k], (k_r, q_r)[kind].at[k], {"seq": up if way == 0 else down})

    def z_send(kind):
        for part in range(PIECES[kind]):
            for way in range(2):
                z_one(kind, way, 1, part)

    def z_step(kind, step):
        for part in range(PIECES[kind]):
            for way in range(2):
                if z_used(kind, way, step, part):
                    z_copies[(kind, step - 1, way, part)].wait_recv()
                    if step < last and z_used(kind, way, step + 1, part):
                        z_one(kind, way, step + 1, part)

    yl1 = 1 - yl
    z_send(0)
    y0 = send(a_buf.at[0, yl, rows_a], a_buf.at[0, yl, rows_a], y_s.at[0], y_r.at[0], yp)
    r0 = send(a_buf.at[0, yl, rows_a], a_buf.at[3, yl, rows_a], x_s.at[0], x_r.at[0], rt)
    l0 = send(a_buf.at[0, yl, rows_b], a_buf.at[1, yl, rows_b], x_s.at[1], x_r.at[1], lf)
    y1 = send(a_buf.at[0, yl, rows_b], a_buf.at[0, yl, rows_b], y_s.at[1], y_r.at[1], yp)
    r1 = send(a_buf.at[0, yl, rows_b], a_buf.at[3, yl, rows_b], x_s.at[2], x_r.at[2], rt)
    l1 = send(a_buf.at[0, yl, rows_a], a_buf.at[1, yl, rows_a], x_s.at[3], x_r.at[3], lf)
    late = []

    place = (z * length + lax.broadcasted_iota(jnp.int32, (length, HD), 0)).astype(F32)
    angle = place * (0.5 * math.pi / (nseq * length))
    trig[0] = jnp.cos(angle)
    trig[1] = jnp.sin(angle)

    for step in range(1, last + 1):
        z_step(0, step)
        if step == QSTART:
            z_send(1)
        if step > QSTART:
            z_step(1, step - QSTART)
        if step == 2:
            r0.wait_recv()
            rf = send(a_buf.at[3, yl, rows_a], a_buf.at[2, yl, rows_a], x_s.at[4], x_r.at[4], rt)
            l0.wait_recv()
            lfw = send(a_buf.at[1, yl, rows_b], a_buf.at[2, yl, rows_b], x_s.at[5], x_r.at[5], lf)
        if step == 4:
            y0.wait_recv()
            y1.wait_recv()
            late.append(send(a_buf.at[0, yl1], a_buf.at[3, yl1], x_s.at[6], x_r.at[6], rt))
            late.append(send(a_buf.at[0, yl1], a_buf.at[1, yl1], x_s.at[7], x_r.at[7], lf))
        if step == 6:
            rf.wait_recv()
            late.append(send(a_buf.at[2, yl, rows_a], a_buf.at[2, yl, rows_a], y_s.at[2], y_r.at[2], yp))
            lfw.wait_recv()
            late.append(send(a_buf.at[2, yl, rows_b], a_buf.at[2, yl, rows_b], y_s.at[3], y_r.at[3], yp))
    q_steps = list(range(last - QSTART + 1, last + 1))

    def q_step():
        if q_steps:
            z_step(1, q_steps.pop(0))

    r1.wait_recv()
    l1.wait_recv()

    def part_of(owner, yb, w):
        return dot(a_buf[lax.rem(owner + NX - x, NX), yb], w[...])

    core_peer = {"col": c1}
    far_peer = {"col": c2}
    halves = (yl, yl1)

    def reduce_far(t, k, w, cs, cr, ys, yr, between):
        cs[t, 0] = part_of(c3, halves[t], w).astype(BF)
        near = send(cs.at[t, 0], cr.at[t, 0], c_s.at[k, t, 0], c_r.at[k, t, 0], core_peer)
        total = part_of(c2, halves[t], w)
        between()
        near.wait_recv()
        ys[t] = (total + cr[t, 0].astype(F32)).astype(BF)
        return send(ys.at[t], yr.at[t], h_s.at[k, t], h_r.at[k, t], far_peer)

    def reduce_near(t, k, w, cs, cr, acc):
        cs[t, 1] = part_of(c1, halves[t], w).astype(BF)
        near = send(cs.at[t, 1], cr.at[t, 1], c_s.at[k, t, 1], c_r.at[k, t, 1], core_peer)
        acc[t] = part_of(c, halves[t], w)
        return near

    nothing = lambda: None
    kv_far, kv_near, q_far, q_near = [], [], [], []
    kv_far.append(reduce_far(0, 0, wkv, cs_kv, cr_kv, ys_kv, yr_kv, nothing))
    q_step()
    kv_near.append(reduce_near(0, 0, wkv, cs_kv, cr_kv, acc_k))
    q_step()
    for cp in late:
        cp.wait_recv()
    kv_far.append(reduce_far(1, 0, wkv, cs_kv, cr_kv, ys_kv, yr_kv, q_step))
    kv_near.append(reduce_near(1, 0, wkv, cs_kv, cr_kv, acc_k))
    while q_steps:
        q_step()

    block = 2 * HD + 2 * NORM
    ones = jnp.ones((NORM, length), BF)

    def states(t):
        kv_near[t].wait_recv()
        kv_far[t].wait_recv()
        yb = halves[t]
        pkv[t] = (acc_k[t] + cr_kv[t, 1].astype(F32) + yr_kv[t].astype(F32)).astype(BF)
        cosine, sine = trig[0], trig[1]
        for h in range(heads):
            i = yb * heads + h
            key = jnp.maximum(pkv[t, :, 2 * h * HD:(2 * h + 1) * HD].astype(F32), 0.0)
            val = pkv[t, :, (2 * h + 1) * HD:(2 * h + 2) * HD]
            kc, ks = (key * cosine).astype(BF), (key * sine).astype(BF)
            kf_buf[i, :, :HD] = kc
            kf_buf[i, :, HD:] = ks
            vx_buf[i, :, :HD] = val
            vx_buf[i, :, HD:] = jnp.ones((length, HD), BF)
            own[i, :HD] = dot(kc, val, ((0,), (0,)))
            own[i, HD:2 * HD] = dot(ks, val, ((0,), (0,)))
            own[i, 2 * HD:2 * HD + NORM] = dot(ones, kc)
            own[i, 2 * HD + NORM:] = dot(ones, ks)

    states(0)
    states(1)

    per = block // CHUNK
    give = remote(own, own0, o_s.at[0], o_r.at[0], core_peer)

    @pl.when(core == 0)
    def _():
        give.start()

    def rows_of(k):
        return pl.ds(pl.multiple_of(k * CHUNK, CHUNK), CHUNK)

    def hop(s, i, k):
        return remote(ob.at[s, i, rows_of(k)], (rb, rb0)[s].at[i, rows_of(k)], p_s.at[s, i, k], p_r.at[s, i, k], {"seq": up})

    def hand(i, k):
        return remote(rb0.at[i, rows_of(k)], rb.at[i, rows_of(k)], f_s.at[i, k], f_r.at[i, k], core_peer)

    def final(i):
        b, h = i // heads, lax.rem(i, heads)
        qf = qf_buf[i]
        num = nd_buf[i, :, :HD] + dot(qf, rb[i, :2 * HD])
        tail = rb[i, 2 * HD:].astype(F32)
        nrm = jnp.concatenate(
            [jnp.broadcast_to(tail[0:1], (HD, HD)), jnp.broadcast_to(tail[NORM:NORM + 1], (HD, HD))], axis=1).astype(BF)
        den = nd_buf[i, :, HD:] + dot(qf, nrm, ((1,), (1,)))
        out[b, :, pl.ds(pl.multiple_of(h * HD, HD), HD)] = (num / jnp.maximum(den, 1.0)).astype(BF)

    def link(s, i):
        into, mine_s = ((rb, own), (rb0, own0))[s]

        @pl.loop(0, per)
        def _(k):
            rows = rows_of(k)

            @pl.when(z == 0)
            def _():
                ob[s, i, rows] = mine_s[i, rows].astype(BF)
                hop(s, i, k).start()

            @pl.when(z > 0)
            def _():
                hop(s, i, k).wait_recv()

                @pl.when(z < nseq - 1)
                def _():
                    ob[s, i, rows] = (into[i, rows].astype(F32) + mine_s[i, rows]).astype(BF)
                    hop(s, i, k).start()

                if s == 1:
                    hand(i, k).start()

    def chain():
        @pl.when(core == 1)
        def _():
            @pl.loop(0, pairs)
            def _(i):
                link(0, i)

            give.wait_recv()

            @pl.loop(0, pairs)
            def _(i):
                link(1, i)

                @pl.when(z == nseq - 1)
                def _():
                    final(i)

    @pl.when(z == 0)
    def _():
        rb[...] = jnp.zeros(rb.shape, BF)

    @pl.when(z < EARLY)
    def _():
        chain()

    for t in range(2):
        q_far.append(reduce_far(t, 1, wq, cs_q, cr_q, ys_q, yr_q, nothing))
    for t in range(2):
        q_near.append(reduce_near(t, 1, wq, cs_q, cr_q, acc_q))
    ii = lax.broadcasted_iota(jnp.int32, (length, length), 0)
    jj = lax.broadcasted_iota(jnp.int32, (length, length), 1)
    causal = jj <= ii
    for t in range(2):
        q_near[t].wait_recv()
        q_far[t].wait_recv()
        for h in range(heads):
            i = halves[t] * heads + h
            cols = slice(h * HD, (h + 1) * HD)
            q = acc_q[t, :, cols] + cr_q[t, 1, :, cols].astype(F32) + yr_q[t, :, cols].astype(F32)
            q = jnp.maximum(q.astype(BF).astype(F32), 0.0)
            qf_buf[i, :, :HD] = (q * trig[0] * HD ** -0.5).astype(BF)
            qf_buf[i, :, HD:] = (q * trig[1] * HD ** -0.5).astype(BF)
            s = dot(qf_buf[i], kf_buf[i], ((1,), (1,)))
            wts = jnp.where(causal, s, 0.0).astype(BF)
            nd_buf[i] = dot(wts, vx_buf[i])

    @pl.when(z >= EARLY)
    def _():
        chain()

    @pl.when((core == 0) | (z < nseq - 1))
    def _():
        @pl.loop(0, pairs)
        def _(i):
            @pl.when((core == 0) & (z > 0))
            def _():
                @pl.loop(0, per)
                def _(k):
                    hand(i, k).wait_recv()

            final(i)

    for cp in sent:
        cp.wait_send()

    @pl.when(core == 0)
    def _():
        give.wait_send()

    @pl.when(core == 1)
    def _():
        @pl.loop(0, pairs)
        def _(i):
            @pl.loop(0, per)
            def _(k):
                @pl.when(z < nseq - 1)
                def _():
                    hop(0, i, k).wait_send()
                    hop(1, i, k).wait_send()

                @pl.when(z > 0)
                def _():
                    hand(i, k).wait_send()


def body(nseq, hidden_in, projection):
    length, depth = hidden_in.shape[1:]
    shard, width = projection.shape
    heads = width // (3 * HD)
    nkv, nq = 2 * heads * HD, heads * HD
    pairs = 2 * heads
    block = 2 * HD + 2 * NORM
    vm, dma = pltpu.VMEM, pltpu.SemaphoreType.DMA
    anywhere = pl.BlockSpec(memory_space=pl.ANY)
    per = block // CHUNK
    wide = (pairs, length, 2 * HD)
    return pl.pallas_call(
        functools.partial(kernel, nseq),
        out_shape=jax.ShapeDtypeStruct((2, length, nq), BF),
        in_specs=[anywhere, anywhere],
        out_specs=pl.BlockSpec(memory_space=pltpu.VMEM),
        scratch_shapes=[
            vm((NX, 2, length, depth), BF), vm((nseq * shard, nkv), BF), vm((nseq * shard, nq), BF),
            vm((2, length, nkv), F32), vm((2, length, nq), F32),
            vm((2, 2, length, nkv), BF), vm((2, 2, length, nq), BF), vm((2, 2, length, nkv), BF), vm((2, 2, length, nq), BF),
            vm((2, length, nkv), BF), vm((2, length, nq), BF), vm((2, length, nkv), BF), vm((2, length, nq), BF),
            vm((2, length, HD), F32), vm((2, length, nkv), BF),
            vm(wide, BF), vm(wide, BF), vm(wide, BF), vm(wide, F32),
            vm((pairs, block, HD), F32), vm((pairs, block, HD), F32),
            vm((pairs, block, HD), BF), vm((pairs, block, HD), BF), vm((2, pairs, block, HD), BF),
            dma((1 + 2 * heads,)), dma((4,)), dma((4,)), dma((8,)), dma((8,)),
            dma((nseq // 2, 2, PIECES[0])), dma((nseq // 2, 2, PIECES[0])),
            dma((nseq // 2, 2, PIECES[1])), dma((nseq // 2, 2, PIECES[1])),
            dma((2, 2, 2)), dma((2, 2, 2)), dma((2, 2)), dma((2, 2)),
            dma((2, pairs, per)), dma((2, pairs, per)), dma((1,)), dma((1,)), dma((pairs, per)), dma((pairs, per)),
        ],
        compiler_params=pltpu.CompilerParams(
            collective_id=0, has_side_effects=True, vmem_limit_bytes=58 * 1024 * 1024),
    )(hidden_in, projection)


def solution(mesh):
    placed = (P("row", "seq", "col"), P(("col", "seq"), "row"))
    return jax.shard_map(
        functools.partial(body, mesh.shape["seq"]), mesh=mesh, in_specs=placed,
        out_specs=P("col", "seq", "row"), check_vma=False)
```

```python
import functools
import math

import jax
import jax.numpy as jnp
from jax import lax
from jax.experimental import pallas as pl
from jax.experimental.pallas import tpu as pltpu
from jax.sharding import PartitionSpec as P

HD = 128
NX = 4
CHUNK = 96
NORM = 16
QSTART = 5
EARLY = 8
SPLIT = 4
MEET = 11
PIECES = (6, 2)
MESH = pl.DeviceIdType.MESH
BF = jnp.bfloat16
F32 = jnp.float32


def dot(a, b, dims=((1,), (0,))):
    return lax.dot_general(a, b, (dims, ((), ())), preferred_element_type=F32)


def kernel(
    nseq, hid, proj, out,
    a_buf, wkv, wq, acc_k, acc_q, cs_kv, cs_q, cr_kv, cr_q, ys_kv, ys_q, yr_kv, yr_q,
    trig, pkv, kf_buf, vx_buf, qf_buf, nd_buf, own, own0, rb, ob, fin,
    loc, y_s, y_r, x_s, x_r, k_s, k_r, q_s, q_r, c_s, c_r, h_s, h_r, p_s, p_r, o_s, o_r, f_s, f_r,
):
    length = hid.shape[1]
    half = length // 2
    shard = proj.shape[0]
    heads = proj.shape[1] // (3 * HD)
    pairs = 2 * heads
    r = lax.axis_index("row")
    c = lax.axis_index("col")
    z = lax.axis_index("seq")
    x, yl = r // 2, r % 2
    yh, core = c // 2, c % 2
    right = lax.rem(x + 1, NX) * 2 + yl
    left = lax.rem(x + NX - 1, NX) * 2 + yl
    ypart = x * 2 + (1 - yl)
    up = lax.rem(z + 1, nseq)
    down = lax.rem(z + nseq - 1, nseq)
    c1 = 2 * yh + (1 - core)
    c2 = 2 * (1 - yh) + core
    c3 = 2 * (1 - yh) + (1 - core)

    loads = [pltpu.make_async_copy(hid.at[0], a_buf.at[0, yl], loc.at[0])]
    mine = pl.ds(pl.multiple_of(z * shard, shard), shard)
    for h in range(heads):
        loads.append(pltpu.make_async_copy(
            proj.at[:, (3 * h + 1) * HD:(3 * h + 3) * HD], wkv.at[mine, 2 * h * HD:2 * (h + 1) * HD], loc.at[1 + 2 * h]))
        loads.append(pltpu.make_async_copy(
            proj.at[:, 3 * h * HD:(3 * h + 1) * HD], wq.at[mine, h * HD:(h + 1) * HD], loc.at[2 + 2 * h]))
    for ld in loads:
        ld.start()

    barrier = pltpu.get_barrier_semaphore()
    peers = [{"row": right}, {"row": left}, {"row": ypart}, {"seq": up}, {"seq": down}, {"col": c1}, {"col": c2}]
    for peer in peers:
        pl.semaphore_signal(barrier, inc=1, device_id=peer, device_id_type=MESH)
    for ld in loads:
        ld.wait()
    pl.semaphore_wait(barrier, len(peers))

    sent = []

    def remote(src, dst, s_sem, r_sem, peer):
        return pltpu.make_async_remote_copy(src_ref=src, dst_ref=dst, send_sem=s_sem, recv_sem=r_sem,
                                            device_id=peer, device_id_type=MESH)

    def send(*what):
        cp = remote(*what)
        cp.start()
        sent.append(cp)
        return cp

    rows_a, rows_b = slice(0, half), slice(half, length)
    yp = {"row": ypart}
    rt = {"row": right}
    lf = {"row": left}

    last = nseq // 2
    z_copies = {}

    def z_used(kind, way, step, part):
        return step < last or (part < PIECES[kind] // 2) == (way == 0)

    def z_one(kind, way, step, part):
        size = shard // PIECES[kind]
        owner = lax.rem(z + nseq - (step - 1), nseq) if way == 0 else lax.rem(z + step - 1, nseq)
        ref = (wkv, wq)[kind].at[pl.ds(pl.multiple_of(owner * shard + part * size, size), size)]
        k = (step - 1, way, part)
        z_copies[(kind,) + k] = send(
            ref, ref, (k_s, q_s)[kind].at[k], (k_r, q_r)[kind].at[k], {"seq": up if way == 0 else down})

    def z_send(kind):
        for part in range(PIECES[kind]):
            for way in range(2):
                z_one(kind, way, 1, part)

    def z_step(kind, step):
        for part in range(PIECES[kind]):
            for way in range(2):
                if z_used(kind, way, step, part):
                    z_copies[(kind, step - 1, way, part)].wait_recv()
                    if step < last and z_used(kind, way, step + 1, part):
                        z_one(kind, way, step + 1, part)

    yl1 = 1 - yl
    z_send(0)
    y0 = send(a_buf.at[0, yl, rows_a], a_buf.at[0, yl, rows_a], y_s.at[0], y_r.at[0], yp)
    r0 = send(a_buf.at[0, yl, rows_a], a_buf.at[3, yl, rows_a], x_s.at[0], x_r.at[0], rt)
    l0 = send(a_buf.at[0, yl, rows_b], a_buf.at[1, yl, rows_b], x_s.at[1], x_r.at[1], lf)
    y1 = send(a_buf.at[0, yl, rows_b], a_buf.at[0, yl, rows_b], y_s.at[1], y_r.at[1], yp)
    r1 = send(a_buf.at[0, yl, rows_b], a_buf.at[3, yl, rows_b], x_s.at[2], x_r.at[2], rt)
    l1 = send(a_buf.at[0, yl, rows_a], a_buf.at[1, yl, rows_a], x_s.at[3], x_r.at[3], lf)
    late = []

    place = (z * length + lax.broadcasted_iota(jnp.int32, (length, HD), 0)).astype(F32)
    angle = place * (0.5 * math.pi / (nseq * length))
    trig[0] = jnp.cos(angle)
    trig[1] = jnp.sin(angle)

    for step in range(1, last + 1):
        z_step(0, step)
        if step == QSTART:
            z_send(1)
        if step > QSTART:
            z_step(1, step - QSTART)
        if step == 2:
            r0.wait_recv()
            rf = send(a_buf.at[3, yl, rows_a], a_buf.at[2, yl, rows_a], x_s.at[4], x_r.at[4], rt)
            l0.wait_recv()
            lfw = send(a_buf.at[1, yl, rows_b], a_buf.at[2, yl, rows_b], x_s.at[5], x_r.at[5], lf)
        if step == 4:
            y0.wait_recv()
            y1.wait_recv()
            late.append(send(a_buf.at[0, yl1], a_buf.at[3, yl1], x_s.at[6], x_r.at[6], rt))
            late.append(send(a_buf.at[0, yl1], a_buf.at[1, yl1], x_s.at[7], x_r.at[7], lf))
        if step == 6:
            rf.wait_recv()
            late.append(send(a_buf.at[2, yl, rows_a], a_buf.at[2, yl, rows_a], y_s.at[2], y_r.at[2], yp))
            lfw.wait_recv()
            late.append(send(a_buf.at[2, yl, rows_b], a_buf.at[2, yl, rows_b], y_s.at[3], y_r.at[3], yp))
    q_steps = list(range(last - QSTART + 1, last + 1))

    def q_step():
        if q_steps:
            z_step(1, q_steps.pop(0))

    r1.wait_recv()
    l1.wait_recv()

    def part_of(owner, yb, w):
        return dot(a_buf[lax.rem(owner + NX - x, NX), yb], w[...])

    core_peer = {"col": c1}
    far_peer = {"col": c2}
    halves = (yl, yl1)

    def reduce_far(t, k, w, cs, cr, ys, yr, between):
        cs[t, 0] = part_of(c3, halves[t], w).astype(BF)
        near = send(cs.at[t, 0], cr.at[t, 0], c_s.at[k, t, 0], c_r.at[k, t, 0], core_peer)
        total = part_of(c2, halves[t], w)
        between()
        near.wait_recv()
        ys[t] = (total + cr[t, 0].astype(F32)).astype(BF)
        return send(ys.at[t], yr.at[t], h_s.at[k, t], h_r.at[k, t], far_peer)

    def reduce_near(t, k, w, cs, cr, acc):
        cs[t, 1] = part_of(c1, halves[t], w).astype(BF)
        near = send(cs.at[t, 1], cr.at[t, 1], c_s.at[k, t, 1], c_r.at[k, t, 1], core_peer)
        acc[t] = part_of(c, halves[t], w)
        return near

    nothing = lambda: None
    kv_far, kv_near, q_far, q_near = [], [], [], []
    kv_far.append(reduce_far(0, 0, wkv, cs_kv, cr_kv, ys_kv, yr_kv, nothing))
    q_step()
    kv_near.append(reduce_near(0, 0, wkv, cs_kv, cr_kv, acc_k))
    q_step()
    for cp in late:
        cp.wait_recv()
    kv_far.append(reduce_far(1, 0, wkv, cs_kv, cr_kv, ys_kv, yr_kv, q_step))
    kv_near.append(reduce_near(1, 0, wkv, cs_kv, cr_kv, acc_k))
    block = 2 * HD + 2 * NORM
    ones = jnp.ones((NORM, length), BF)

    def states(t):
        kv_near[t].wait_recv()
        kv_far[t].wait_recv()
        pkv[t] = (acc_k[t] + cr_kv[t, 1].astype(F32) + yr_kv[t].astype(F32)).astype(BF)
        cosine, sine = trig[0], trig[1]
        for h in range(heads):
            i = t * heads + h
            key = jnp.maximum(pkv[t, :, 2 * h * HD:(2 * h + 1) * HD].astype(F32), 0.0)
            val = pkv[t, :, (2 * h + 1) * HD:(2 * h + 2) * HD]
            kc, ks = (key * cosine).astype(BF), (key * sine).astype(BF)
            kf_buf[i, :, :HD] = kc
            kf_buf[i, :, HD:] = ks
            vx_buf[i, :, :HD] = val
            vx_buf[i, :, HD:] = jnp.ones((length, HD), BF)
            own[i, :HD] = dot(kc, val, ((0,), (0,)))
            own[i, HD:2 * HD] = dot(ks, val, ((0,), (0,)))
            own[i, 2 * HD:2 * HD + NORM] = dot(ones, kc)
            own[i, 2 * HD + NORM:] = dot(ones, ks)

        @pl.when((core == 0) | (z < SPLIT))
        def _():
            give(t).start()

    per = block // CHUNK

    def give(t):
        these = pl.ds(t * heads, heads)
        return remote(own.at[these], own0.at[these], o_s.at[t], o_r.at[t], core_peer)

    def rows_of(k):
        return pl.ds(pl.multiple_of(k * CHUNK, CHUNK), CHUNK)

    def hop(f, s, i, k, way, src):
        rows = rows_of(k)
        return remote(src.at[f, s, i, rows], rb.at[f, s, i, rows], p_s.at[f, s, i, k], p_r.at[f, s, i, k], {"seq": way})

    def hand(f, i, k):
        rows = rows_of(k)
        return remote(rb.at[f, 1, i, rows], rb.at[2, 0, i, rows], f_s.at[i, k], f_r.at[i, k], core_peer)

    def chunks(t, do):
        @pl.loop(0, heads)
        def _(h):
            @pl.loop(0, per)
            def _(k):
                do(t * heads + h, k)

    flow = (z >= SPLIT).astype(jnp.int32)
    origin = (z == 0) | (z == SPLIT)

    def relay(f, s, i, k, way, first):
        rows = rows_of(k)
        mine_s = (own, own0)[s]

        @pl.when(first)
        def _():
            ob[f, s, i, rows] = mine_s[i, rows].astype(BF)

        @pl.when(jnp.logical_not(first))
        def _():
            ob[f, s, i, rows] = (rb[f, s, i, rows].astype(F32) + mine_s[i, rows]).astype(BF)

        hop(f, s, i, k, way, ob).start()

    def first_up(t):
        for s in range(2):
            if s == 1:
                give(t).wait_recv()

            def do(i, k):
                @pl.when(jnp.logical_not(origin))
                def _():
                    hop(flow, s, i, k, up, ob).wait_recv()

                @pl.when(z < nseq - 1)
                def _():
                    relay(flow, s, i, k, up, origin)

                if s == 1:
                    @pl.when(((z > 0) & (z < SPLIT)) | (z > MEET))
                    def _():
                        hand(flow, i, k).start()

            chunks(t, do)

    def second_up(t):
        for s in range(2):
            def do(i, k):
                hop(0, s, i, k, up, ob).wait_recv()

                @pl.when(z < MEET)
                def _():
                    relay(0, s, i, k, up, False)

                if s == 1:
                    hand(0, i, k).start()

            chunks(t, do)

    def around(t):
        for s in range(2):
            if s == 1:
                @pl.when(z < SPLIT)
                def _():
                    give(t).wait_recv()

            def do(i, k):
                @pl.when(z != SPLIT - 1)
                def _():
                    hop(0, s, i, k, down, ob).wait_recv()

                @pl.when(z < SPLIT)
                def _():
                    relay(0, s, i, k, down, z == SPLIT - 1)

                @pl.when(z > MEET + 1)
                def _():
                    hop(0, s, i, k, down, rb).start()

                if s == 1:
                    @pl.when(z > MEET)
                    def _():
                        hand(0, i, k).start()

            chunks(t, do)

    def chain(t):
        @pl.when(core == 1)
        def _():
            first_up(t)

        @pl.when((core == 0) & ((z < SPLIT) | (z > MEET)))
        def _():
            around(t)

    def chain_on():
        @pl.when((core == 1) & (z >= SPLIT) & (z <= MEET))
        def _():
            second_up(0)
            second_up(1)

    while q_steps:
        q_step()
    for t in range(2):
        q_far.append(reduce_far(t, 1, wq, cs_q, cr_q, ys_q, yr_q, nothing))
    for t in range(2):
        q_near.append(reduce_near(t, 1, wq, cs_q, cr_q, acc_q))

    f1 = jnp.where(core == 0, 2, (z > MEET).astype(jnp.int32))
    f2 = jnp.where(core == 0, 0, 2)

    @pl.when(z == 0)
    def _():
        rb[f1, 0] = jnp.zeros(rb.shape[2:], BF)

    early = jnp.where(core == 1, z < EARLY, z < SPLIT)
    states(0)

    states(1)

    @pl.when(early)
    def _():
        chain(0)
        chain(1)
        chain_on()

    ii = lax.broadcasted_iota(jnp.int32, (length, length), 0)
    jj = lax.broadcasted_iota(jnp.int32, (length, length), 1)
    causal = jj <= ii
    for t in range(2):
        q_near[t].wait_recv()
        q_far[t].wait_recv()
        for h in range(heads):
            i = t * heads + h
            cols = slice(h * HD, (h + 1) * HD)
            q = acc_q[t, :, cols] + cr_q[t, 1, :, cols].astype(F32) + yr_q[t, :, cols].astype(F32)
            q = jnp.maximum(q.astype(BF).astype(F32), 0.0)
            qf_buf[i, :, :HD] = (q * trig[0] * HD ** -0.5).astype(BF)
            qf_buf[i, :, HD:] = (q * trig[1] * HD ** -0.5).astype(BF)
            s = dot(qf_buf[i], kf_buf[i], ((1,), (1,)))
            wts = jnp.where(causal, s, 0.0).astype(BF)
            nd_buf[i] = dot(wts, vx_buf[i])

    @pl.when(jnp.logical_not(early))
    def _():
        chain(0)
        chain(1)
        chain_on()

    @pl.loop(0, pairs)
    def _(i):
        @pl.when(((core == 0) & (z > 0)) | (z > MEET))
        def _():
            @pl.loop(0, per)
            def _(k):
                hand(0, i, k).wait_recv()

        @pl.when(z <= MEET)
        def _():
            fin[...] = rb[f1, 0, i]

        @pl.when(z > MEET)
        def _():
            fin[...] = (rb[f1, 0, i].astype(F32) + rb[f2, 0, i].astype(F32)).astype(BF)

        b, h = lax.rem(i // heads + yl, 2), lax.rem(i, heads)
        qf = qf_buf[i]
        num = nd_buf[i, :, :HD] + dot(qf, fin[:2 * HD])
        ends = fin[2 * HD:].astype(F32)
        nrm = jnp.concatenate(
            [jnp.broadcast_to(ends[0:1], (HD, HD)), jnp.broadcast_to(ends[NORM:NORM + 1], (HD, HD))], axis=1).astype(BF)
        den = nd_buf[i, :, HD:] + dot(qf, nrm, ((1,), (1,)))
        out[b, :, pl.ds(pl.multiple_of(h * HD, HD), HD)] = (num / jnp.maximum(den, 1.0)).astype(BF)

    for cp in sent:
        cp.wait_send()

    for t in range(2):
        @pl.when((core == 0) | (z < SPLIT))
        def _():
            give(t).wait_send()

    @pl.loop(0, pairs)
    def _(i):
        @pl.loop(0, per)
        def _(k):
            for s in range(2):
                @pl.when((core == 1) & (z < nseq - 1))
                def _():
                    hop(flow, s, i, k, up, ob).wait_send()

                @pl.when((core == 1) & (z >= SPLIT) & (z < MEET))
                def _():
                    hop(0, s, i, k, up, ob).wait_send()

                @pl.when((core == 0) & ((z < SPLIT) | (z > MEET + 1)))
                def _():
                    hop(0, s, i, k, down, ob).wait_send()

            @pl.when(((core == 1) & (z > 0)) | ((core == 0) & (z > MEET)))
            def _():
                hand(0, i, k).wait_send()


def body(nseq, hidden_in, projection):
    length, depth = hidden_in.shape[1:]
    shard, width = projection.shape
    heads = width // (3 * HD)
    nkv, nq = 2 * heads * HD, heads * HD
    pairs = 2 * heads
    block = 2 * HD + 2 * NORM
    vm, dma = pltpu.VMEM, pltpu.SemaphoreType.DMA
    anywhere = pl.BlockSpec(memory_space=pl.ANY)
    per = block // CHUNK
    wide = (pairs, length, 2 * HD)
    return pl.pallas_call(
        functools.partial(kernel, nseq),
        out_shape=jax.ShapeDtypeStruct((2, length, nq), BF),
        in_specs=[anywhere, anywhere],
        out_specs=pl.BlockSpec(memory_space=pltpu.VMEM),
        scratch_shapes=[
            vm((NX, 2, length, depth), BF), vm((nseq * shard, nkv), BF), vm((nseq * shard, nq), BF),
            vm((2, length, nkv), F32), vm((2, length, nq), F32),
            vm((2, 2, length, nkv), BF), vm((2, 2, length, nq), BF), vm((2, 2, length, nkv), BF), vm((2, 2, length, nq), BF),
            vm((2, length, nkv), BF), vm((2, length, nq), BF), vm((2, length, nkv), BF), vm((2, length, nq), BF),
            vm((2, length, HD), F32), vm((2, length, nkv), BF),
            vm(wide, BF), vm(wide, BF), vm(wide, BF), vm(wide, F32),
            vm((pairs, block, HD), F32), vm((pairs, block, HD), F32),
            vm((3, 2, pairs, block, HD), BF), vm((2, 2, pairs, block, HD), BF), vm((block, HD), BF),
            dma((1 + 2 * heads,)), dma((4,)), dma((4,)), dma((8,)), dma((8,)),
            dma((nseq // 2, 2, PIECES[0])), dma((nseq // 2, 2, PIECES[0])),
            dma((nseq // 2, 2, PIECES[1])), dma((nseq // 2, 2, PIECES[1])),
            dma((2, 2, 2)), dma((2, 2, 2)), dma((2, 2)), dma((2, 2)),
            dma((2, 2, pairs, per)), dma((2, 2, pairs, per)), dma((2,)), dma((2,)), dma((pairs, per)), dma((pairs, per)),
        ],
        compiler_params=pltpu.CompilerParams(
            collective_id=0, has_side_effects=True, vmem_limit_bytes=58 * 1024 * 1024),
    )(hidden_in, projection)


def solution(mesh):
    placed = (P("row", "seq", "col"), P(("col", "seq"), "row"))
    return jax.shard_map(
        functools.partial(body, mesh.shape["seq"]), mesh=mesh, in_specs=placed,
        out_specs=P("col", "seq", "row"), check_vma=False)
```
